32 devices in a mesh: chan: 2 (over x), cyl: 4 (over z), tm: 4 (over y, core).
Axes of the slice: x: 2, y: 2, z: 4, core: 2. Of those that a mesh axis runs over, the one named last changes fastest.
Arguments:
- voltages: bfloat16 [8, 4, 2, 2, 256, 2048], P('chan', 'cyl', None, None, None, 'tm'), may hold values from -6 to 6
- feed_gains: float32 [8, 4, 2, 2, 256], P('chan', 'cyl'), may hold values from -8 to 8
- grid_slot: int32 [4, 256], replicated, may hold values from 0 to 511, as said below
- transit_start: int32 [4], replicated, may hold values from 0 to 1024
Outputs:
- beam_map: float32 [8, 4, 512], P('chan', None, ('cyl', 'tm'))
- transit_snr: float32 [4, 4, 512], P(None, None, ('cyl', 'tm'))
The draws below stay inside these ranges and needn't reach their ends.
Inputs may be any that keep to these rules, and one draw needn't show every extreme that they name: `grid_slot`: within each cylinder the 256 grid points are distinct.
All inputs are finite; a program needn't handle non-finite values.
Results may differ from the reference program's by a relative error of at most 0.0031.
Values may be sent and summed in bfloat16 or wider, within the bound.
A program may use at most 64 MiB of HBM per device.

```python
import math
import jax
import jax.numpy as jnp
from jax import lax

FEEDS = 256
CYLS = 4
POLS = 2
NS = 512
CALS = 4
CHANNELS = 8
FRAMES = 2048
WIN = 1024


def draw_feed_gains(key, part):
    keys = jax.random.split(key, 3)
    ramp = jnp.arange(CHANNELS, dtype=jnp.float32) / max(CHANNELS - 1, 1)
    bandpass = jnp.exp(0.5 * math.log(3.0) * ramp + jax.random.uniform(keys[0], (CHANNELS,), jnp.float32, -0.25, 0.25))
    grid_shape = (CHANNELS, CYLS, POLS, FEEDS)
    amplitude = jnp.exp(jax.random.uniform(keys[1], grid_shape, jnp.float32, math.log(0.5), math.log(2.0)))
    phase = jax.random.uniform(keys[2], grid_shape, jnp.float32, -math.pi, math.pi)
    scaled = bandpass[:, None, None, None] * amplitude
    return jnp.stack([scaled * jnp.cos(phase), scaled * jnp.sin(phase)], axis=3).astype(jnp.float32)


def draw_grid_slot(key, part):

    def one_cylinder(cyl_key):
        pair = jax.random.split(cyl_key, 2)
        index = jnp.arange(FEEDS, dtype=jnp.int32)
        parity = jax.random.randint(pair[0], (FEEDS,), 0, 2, dtype=jnp.int32)
        parity = jnp.where(index == 0, 0, jnp.where(index == FEEDS - 1, 1, parity))
        places = 2 * index + parity
        order = jax.random.permutation(pair[1], FEEDS)
        return places[order]
    return jax.vmap(one_cylinder)(jax.random.split(key, CYLS)).astype(jnp.int32)


def with_ends(entries, rng, least, largest):
    longest = entries.shape.index(max(entries.shape))
    spots = []
    for shift in (0, 1):
        where = [jax.random.randint(jax.random.fold_in(rng, axis), (), 0, length) for axis, length in enumerate(entries.shape)]
        where[longest] = (where[longest] + shift) % entries.shape[longest]
        spots.append(tuple(where))
    return entries.at[spots[0]].set(least).at[spots[1]].set(largest)


def levels(own_key, dims, shards, smallest, top_value):
    gain = 1.0
    for position, blocks in shards:
        steps = jax.random.uniform(jax.random.fold_in(jax.random.fold_in(own_key, 6), position), (blocks,), jnp.float32, smallest / len(shards), top_value / len(shards))
        gain = gain * jnp.repeat(jnp.exp(steps), dims[position] // blocks).reshape((-1,) + (1,) * (len(dims) - 1 - position))
    return gain


def gaussian(stream_key, extent, scale, limit, shards=(), held_as=jnp.bfloat16):
    level = levels(stream_key, extent, shards, -0.22, 0.18) if shards else 1.0
    result = jax.random.normal(stream_key, extent, jnp.float32) * scale * level
    return jnp.minimum(jnp.maximum(result, -limit), limit).astype(held_as)


def setup_inputs(seed: int = 0) -> dict:
    splits = jax.random.split(jax.random.key(seed), 5)
    voltages = gaussian(splits[0], (CHANNELS, CYLS, POLS, 2, FEEDS, FRAMES), 1.0, 6.0, ((0, 2), (1, 4), (5, 4)))
    feed_gains = draw_feed_gains(jax.random.fold_in(splits[4], 71), 0)
    grid_slot = draw_grid_slot(jax.random.fold_in(splits[4], 71), 0)
    transit_start = with_ends(jax.random.randint(splits[3], (CALS,), 0, FRAMES - WIN + 1), jax.random.fold_in(splits[3], 1), 0, FRAMES - WIN).astype(jnp.int32)
    return {"voltages": voltages, "feed_gains": feed_gains, "grid_slot": grid_slot, "transit_start": transit_start}


EPSILON = 1e-06

def slot_matrix(grid_slots, grid_size):
    indices = jnp.arange(grid_size, dtype=jnp.int32)
    turns = grid_slots[..., None, :] * indices[:, None] % grid_size
    angle = turns.astype(jnp.float32) * (2.0 * math.pi / grid_size)
    factor = 1.0 / math.sqrt(grid_slots.shape[-1])
    cosine = jnp.cos(angle) * factor
    sine_part = jnp.sin(angle) * factor
    upper = jnp.stack([cosine, sine_part], axis=-2)
    lower = jnp.stack([-sine_part, cosine], axis=-2)
    return jnp.stack([upper, lower], axis=-4).astype(jnp.bfloat16)

def east_west_table(count):
    rows = jnp.arange(count, dtype=jnp.int32)
    quarter = rows[:, None] * rows[None, :] % 4
    cosine = jnp.where(quarter == 0, 1.0, jnp.where(quarter == 2, -1.0, 0.0))
    sine_part = jnp.where(quarter == 1, 1.0, jnp.where(quarter == 3, -1.0, 0.0))
    real_row = jnp.stack([cosine, sine_part], axis=-1)
    imag_row = jnp.stack([-sine_part, cosine], axis=-1)
    return (0.5 * jnp.stack([real_row, imag_row], axis=1)).astype(jnp.bfloat16)

def frame_shapes(starts, offset, count, window):
    frame_index = offset + jnp.arange(count, dtype=jnp.int32)
    relative = frame_index[None, :] - starts[:, None]
    inside = (relative >= 0) & (relative < window)
    wave = jnp.sin(math.pi * (relative.astype(jnp.float32) + 0.5) / window)
    return jnp.where(inside, wave * wave, 0.0).astype(jnp.float32)

def calibrate(voltage, gain_row):
    gain_re = gain_row[..., 0, :, None]
    gain_im = gain_row[..., 1, :, None]
    volt_re = voltage[..., 0, :, :]
    volt_im = voltage[..., 1, :, :]
    real_part = gain_re * volt_re - gain_im * volt_im
    imag_part = gain_re * volt_im + gain_im * volt_re
    return jnp.stack([real_part, imag_part], axis=-3).astype(jnp.bfloat16)

def beam_moments(spectra, shapes):
    table = east_west_table(spectra.shape[0]).astype(jnp.float32)
    formed = jnp.einsum('cprmf,eocr->epomf', spectra.astype(jnp.float32), table, precision=lax.Precision.HIGHEST)
    power = lax.optimization_barrier(jnp.sum(formed * formed, axis=(1, 2)))
    zeroth = lax.optimization_barrier(jnp.sum(power, axis=-1))
    second = lax.optimization_barrier(jnp.sum(power * power, axis=-1))
    cross = jnp.einsum('emf,kf->kem', power, shapes, precision=lax.Precision.HIGHEST)
    return (zeroth, jnp.concatenate([cross, second[None]], axis=0))

def transit_ratio(sums, template_sum, template_sq, channels, frames):
    count_cal = template_sum.shape[0]
    cross = sums[:count_cal]
    second = sums[count_cal]
    zeroth = sums[count_cal + 1]
    samples = channels * frames
    average = zeroth / samples
    variance = second / samples - average * average
    spread = channels * (template_sq - template_sum * template_sum / frames)
    widen = (count_cal,) + (1,) * (cross.ndim - 1)
    numerator = cross - template_sum.reshape(widen) * zeroth / frames
    return numerator / jnp.sqrt(spread.reshape(widen) * (variance + EPSILON))

def reference(voltages, feed_gains, grid_slot, transit_start):
    matrices = slot_matrix(grid_slot, NS).astype(jnp.float32)
    shapes = frame_shapes(transit_start, 0, FRAMES, WIN)

    def one_channel(item):
        voltage, gain_row = item
        calibrated = calibrate(voltage, gain_row).astype(jnp.float32)
        spectra = jnp.einsum('comrs,cprst->cpomt', matrices, calibrated, precision=lax.Precision.HIGHEST)
        return beam_moments(spectra.astype(jnp.bfloat16), shapes)
    zeroth, moments = lax.map(one_channel, (voltages, feed_gains))
    beam_map = zeroth / FRAMES
    sums = jnp.concatenate([lax.optimization_barrier(jnp.sum(moments, axis=0)), lax.optimization_barrier(jnp.sum(zeroth, axis=0))[None]], axis=0)
    template_sum = lax.optimization_barrier(jnp.sum(shapes, axis=1))
    template_sq = lax.optimization_barrier(jnp.sum(shapes * shapes, axis=1))
    transit_snr = transit_ratio(sums, template_sum, template_sq, CHANNELS, FRAMES)
    return (beam_map, transit_snr)
```

```python
import functools
import math

import jax
import jax.numpy as jnp
from jax import lax
from jax.experimental import pallas as pl
from jax.experimental.pallas import tpu as pltpu
from jax.sharding import PartitionSpec as P

NS = 512
EPSILON = 1e-06
MESH = pl.DeviceIdType.MESH
LANES = 128


def slot_tables(slots, rows, size):
    turns = (slots * rows) & (size - 1)
    eighth = size // 8
    quarter = size // 4
    quadrant = (turns + eighth) // quarter
    rest = turns - quadrant * quarter
    x = rest.astype(jnp.float32) * (2.0 * math.pi / size)
    x2 = x * x
    sine = x * (1.0 + x2 * (-1.0 / 6 + x2 * (1.0 / 120 + x2 * (-1.0 / 5040 + x2 * (1.0 / 362880)))))
    cosine = 1.0 + x2 * (-0.5 + x2 * (1.0 / 24 + x2 * (-1.0 / 720 + x2 * (1.0 / 40320))))
    odd = (quadrant & 1) == 1
    c = jnp.where(odd, sine, cosine)
    s = jnp.where(odd, cosine, sine)
    c = jnp.where((quadrant == 1) | (quadrant == 2), -c, c)
    s = jnp.where((quadrant == 2) | (quadrant == 3), -s, s)
    return c, s


def kernel(
    sizes,
    volt,
    gains,
    slots,
    starts,
    map_out,
    snr_out,
    vbuf,
    gbuf,
    gwide,
    table,
    cal,
    spec,
    acc,
    shapes,
    mom_send,
    mom_recv,
    pool_send,
    pool_recv,
    vs_sem,
    vr_sem,
    gs_sem,
    gr_sem,
    ms_sem,
    mr_sem,
    ps_sem,
    pr_sem,
):
    nchan, ncyl, ntm, ch_dev, fr_dev, pols, feeds, ncal = sizes
    chunks = fr_dev // LANES
    frames = fr_dev * ntm
    window = frames // 2
    channels = ch_dev * nchan
    owners = ncyl * ntm
    my_chan = lax.axis_index("chan")
    me = lax.axis_index("cyl")
    my_tm = lax.axis_index("tm")
    mine = me * ntm + my_tm

    near = me + 1 - 2 * (me % 2)
    middle = (me + 2) % ncyl
    mirror = ncyl - 1 - me
    peers = (near, mirror, middle)

    def owner_device(step):
        target = (mine + step) % owners
        return target, {"cyl": target // ntm, "tm": target % ntm}

    def chan_device(step):
        target = (my_chan + step) % nchan
        return target, {"chan": target}

    barrier = pltpu.get_barrier_semaphore()
    for step in range(1, owners):
        pl.semaphore_signal(barrier, inc=1, device_id=owner_device(step)[1], device_id_type=MESH)
    for step in range(1, nchan):
        pl.semaphore_signal(barrier, inc=1, device_id=chan_device(step)[1], device_id_type=MESH)
    pl.semaphore_wait(barrier, owners - 1 + nchan - 1)

    def gain_copy(j):
        return pltpu.make_async_remote_copy(
            src_ref=gains.at[peers[j], 0],
            dst_ref=gbuf.at[me],
            send_sem=gs_sem.at[j],
            recv_sem=gr_sem.at[me],
            device_id={"cyl": peers[j]},
            device_id_type=MESH,
        )

    def volt_copy(j, k):
        return pltpu.make_async_remote_copy(
            src_ref=volt.at[peers[j], 0, :, :, :, pl.ds(k * LANES, LANES)],
            dst_ref=vbuf.at[k, me],
            send_sem=vs_sem.at[j, k],
            recv_sem=vr_sem.at[k, me],
            device_id={"cyl": peers[j]},
            device_id_type=MESH,
        )

    def own_volt(k):
        return pltpu.make_async_copy(
            volt.at[me, 0, :, :, :, pl.ds(k * LANES, LANES)], vbuf.at[k, me], vr_sem.at[k, me]
        )

    own_gain = pltpu.make_async_copy(gains.at[me, 0], gbuf.at[me], gr_sem.at[me])

    for j in range(3):
        gain_copy(j).start()
    own_gain.start()
    for k in range(chunks):
        volt_copy(0, k).start()
    for k in range(chunks):
        volt_copy(1, k).start()
        volt_copy(2, k).start()
    for k in range(chunks):
        own_volt(k).start()

    rows_per = 64

    def build(c, carry):
        slot_row = slots[pl.ds(c, 1), :]

        def block(b, inner):
            base = pl.multiple_of(b * rows_per, rows_per)
            row = lax.broadcasted_iota(jnp.int32, (rows_per, feeds), 0) + base
            cosine, sine = slot_tables(slot_row, row, NS)
            factor = 1.0 / math.sqrt(feeds)
            cosine = (cosine * factor).astype(jnp.bfloat16)
            sine = (sine * factor).astype(jnp.bfloat16)
            table[c, pl.ds(base, rows_per), pl.ds(0, feeds)] = cosine
            table[c, pl.ds(base, rows_per), pl.ds(feeds, feeds)] = sine
            low = pl.multiple_of(base + NS, rows_per)
            table[c, pl.ds(low, rows_per), pl.ds(0, feeds)] = -sine
            table[c, pl.ds(low, rows_per), pl.ds(feeds, feeds)] = cosine
            return inner

        return lax.fori_loop(0, NS // rows_per, block, carry)

    lax.fori_loop(0, ncyl, build, 0)

    def template(first, width, k):
        frame = lax.broadcasted_iota(jnp.int32, (8, width), 1) + first
        relative = frame - starts[k]
        inside = (relative >= 0) & (relative < window)
        wave = jnp.sin(math.pi * (relative.astype(jnp.float32) + 0.5) / window)
        return jnp.where(inside, wave * wave, 0.0)

    tsum = []
    tsq = []
    for k in range(ncal):
        whole = template(0, frames, k)[0:1, :]
        tsum.append(jnp.sum(whole, axis=1, keepdims=True))
        tsq.append(jnp.sum(whole * whole, axis=1, keepdims=True))
        own = template(my_tm * fr_dev, fr_dev, k)
        for t in range(chunks):
            shapes[t, k] = own[:, t * LANES : (t + 1) * LANES]

    acc[...] = jnp.zeros_like(acc)

    for j in range(3):
        gain_copy(j).wait_send()
        pltpu.make_async_remote_copy(
            src_ref=gains.at[peers[j], 0],
            dst_ref=gbuf.at[peers[j]],
            send_sem=gs_sem.at[j],
            recv_sem=gr_sem.at[peers[j]],
            device_id={"cyl": peers[j]},
            device_id_type=MESH,
        ).wait_recv()
    own_gain.wait()
    flat = jnp.concatenate([gbuf[c, p] for c in range(ncyl) for p in range(pols)], axis=0)
    tall = flat.T
    for i in range(ncyl * pols * 2):
        gwide[i] = jnp.broadcast_to(tall[:, i : i + 1], (feeds, LANES))

    def chunk_step(k, carry):
        for j in range(3):
            pltpu.make_async_remote_copy(
                src_ref=volt.at[peers[j], 0, :, :, :, pl.ds(0, LANES)],
                dst_ref=vbuf.at[k, peers[j]],
                send_sem=vs_sem.at[j, k],
                recv_sem=vr_sem.at[k, peers[j]],
                device_id={"cyl": peers[j]},
                device_id_type=MESH,
            ).wait_recv()
        own_volt(k).wait()

        def form(i, inner):
            c = i // pols
            p = i % pols
            gain_re = gwide[2 * i]
            gain_im = gwide[2 * i + 1]
            volt_re = vbuf[k, c, p, 0].astype(jnp.float32)
            volt_im = vbuf[k, c, p, 1].astype(jnp.float32)
            cal[0:feeds, :] = (gain_re * volt_re - gain_im * volt_im).astype(jnp.bfloat16)
            cal[feeds : 2 * feeds, :] = (gain_re * volt_im + gain_im * volt_re).astype(jnp.bfloat16)
            spec[i] = jnp.dot(table[c], cal[...], preferred_element_type=jnp.float32).astype(
                jnp.bfloat16
            )
            return inner

        lax.fori_loop(0, ncyl * pols, form, 0)

        rows = 16
        span = NS // owners

        def beams(b, inner):
            base = pl.multiple_of(b * rows, rows)
            owner = b // (span // rows)
            part = (b % (span // rows)) * rows
            power = [None] * 4
            for p in range(pols):
                re = []
                im = []
                for c in range(4):
                    re.append(spec[c * pols + p, pl.ds(base, rows), :].astype(jnp.float32))
                    low = pl.multiple_of(base + NS, rows)
                    im.append(spec[c * pols + p, pl.ds(low, rows), :].astype(jnp.float32))
                re_even, re_odd = re[0] + re[2], re[1] + re[3]
                im_even, im_odd = im[0] + im[2], im[1] + im[3]
                re_alt, im_alt = re[0] - re[2], im[0] - im[2]
                re_skew, im_skew = re[1] - re[3], im[1] - im[3]
                formed = (
                    (re_even + re_odd, im_even + im_odd),
                    (re_alt + im_skew, im_alt - re_skew),
                    (re_even - re_odd, im_even - im_odd),
                    (re_alt - im_skew, im_alt + re_skew),
                )
                for e in range(4):
                    square = formed[e][0] * formed[e][0] + formed[e][1] * formed[e][1]
                    power[e] = square if power[e] is None else power[e] + square
            for e in range(4):
                value = 0.25 * power[e]
                where = pl.ds(pl.multiple_of(e * span + part, rows), rows)
                acc[0, owner, where, :] += value
                acc[1, owner, where, :] += value * value
                for t in range(ncal):
                    shape = shapes[k, t]
                    acc[2 + t, owner, where, :] += value * jnp.concatenate([shape, shape], axis=0)
            return inner

        return lax.fori_loop(0, NS // rows, beams, carry)

    lax.fori_loop(0, chunks, chunk_step, 0)

    lane = lax.broadcasted_iota(jnp.int32, (LANES, LANES), 1)

    def gather(d, carry):
        merged = jnp.zeros((LANES, LANES), jnp.float32)
        for i in range(2 + ncal):
            total = jnp.sum(acc[i, d], axis=1, keepdims=True)
            merged = jnp.where(lane == i, total, merged)
        mom_send[d] = merged.T[0:8, :]
        return carry

    lax.fori_loop(0, owners, gather, 0)

    def moment_copy(step, target, place, device):
        return pltpu.make_async_remote_copy(
            src_ref=mom_send.at[target],
            dst_ref=mom_recv.at[place],
            send_sem=ms_sem.at[step],
            recv_sem=mr_sem.at[place],
            device_id=device,
            device_id_type=MESH,
        )

    for step in range(1, owners):
        target, device = owner_device(step)
        moment_copy(step, target, mine, device).start()
    own_moment = pltpu.make_async_copy(mom_send.at[mine], mom_recv.at[mine], mr_sem.at[mine])
    own_moment.start()
    for step in range(1, owners):
        target, device = owner_device(step)
        moment_copy(step, target, target, device).wait_recv()
    own_moment.wait()

    pooled = jnp.zeros((8, LANES), jnp.float32)
    for z in range(ncyl):
        own = mom_recv[z * ntm]
        for t in range(1, ntm):
            own = own + mom_recv[z * ntm + t]
        map_out[z : z + 1, :] = own[0:1, :] / frames
        pooled = pooled + own
    pool_send[...] = pooled

    def pool_copy(step, place, device):
        return pltpu.make_async_remote_copy(
            src_ref=pool_send,
            dst_ref=pool_recv.at[place],
            send_sem=ps_sem.at[step],
            recv_sem=pr_sem.at[place],
            device_id=device,
            device_id_type=MESH,
        )

    for step in range(1, nchan):
        target, device = chan_device(step)
        pool_copy(step, my_chan, device).start()
    for step in range(1, nchan):
        target, device = chan_device(step)
        pool_copy(step, target, device).wait_recv()
        pooled = pooled + pool_recv[target]

    samples = channels * frames
    zeroth = pooled[0:1, :]
    average = zeroth / samples
    variance = pooled[1:2, :] / samples - average * average
    for k in range(ncal):
        spread = channels * (tsq[k] - tsum[k] * tsum[k] / frames)
        numerator = pooled[2 + k : 3 + k, :] - tsum[k] * zeroth / frames
        snr_out[k : k + 1, :] = numerator / jnp.sqrt(spread * (variance + EPSILON))

    for j in range(3):
        for k in range(chunks):
            volt_copy(j, k).wait_send()
    for step in range(1, owners):
        target, device = owner_device(step)
        moment_copy(step, target, mine, device).wait_send()
    for step in range(1, nchan):
        target, device = chan_device(step)
        pool_copy(step, my_chan, device).wait_send()


def per_device(voltages, feed_gains, grid_slot, transit_start):
    ch_dev, _, pols, _, feeds, fr_dev = voltages.shape
    nchan = lax.axis_size("chan")
    ncyl = lax.axis_size("cyl")
    ntm = lax.axis_size("tm")
    ncal = transit_start.shape[0]
    assert ncyl == 4 and ch_dev == ncyl
    chunks = fr_dev // LANES
    owners = ncyl * ntm
    sizes = (nchan, ncyl, ntm, ch_dev, fr_dev, pols, feeds, ncal)
    dma = pltpu.SemaphoreType.DMA
    f32 = jnp.float32
    bf16 = jnp.bfloat16
    beam_map, transit_snr = pl.pallas_call(
        functools.partial(kernel, sizes),
        out_shape=(
            jax.ShapeDtypeStruct((ch_dev, LANES), f32),
            jax.ShapeDtypeStruct((ncal, LANES), f32),
        ),
        in_specs=[
            pl.BlockSpec(memory_space=pl.ANY),
            pl.BlockSpec(memory_space=pl.ANY),
            pl.BlockSpec(memory_space=pltpu.VMEM),
            pl.BlockSpec(memory_space=pltpu.SMEM),
        ],
        out_specs=(
            pl.BlockSpec(memory_space=pltpu.VMEM),
            pl.BlockSpec(memory_space=pltpu.VMEM),
        ),
        scratch_shapes=[
            pltpu.VMEM((chunks, ncyl, pols, 2, feeds, LANES), bf16),
            pltpu.VMEM((ncyl, pols, 2, feeds), f32),
            pltpu.VMEM((ncyl * pols * 2, feeds, LANES), f32),
            pltpu.VMEM((ncyl, 2 * NS, 2 * feeds), bf16),
            pltpu.VMEM((2 * feeds, LANES), bf16),
            pltpu.VMEM((ncyl * pols, 2 * NS, LANES), bf16),
            pltpu.VMEM((2 + ncal, owners, 4 * NS // owners, LANES), f32),
            pltpu.VMEM((chunks, ncal, 8, LANES), f32),
            pltpu.VMEM((owners, 8, LANES), f32),
            pltpu.VMEM((owners, 8, LANES), f32),
            pltpu.VMEM((8, LANES), f32),
            pltpu.VMEM((nchan, 8, LANES), f32),
            dma((3, chunks)),
            dma((chunks, ncyl)),
            dma((3,)),
            dma((ncyl,)),
            dma((owners,)),
            dma((owners,)),
            dma((nchan,)),
            dma((nchan,)),
        ],
        compiler_params=pltpu.CompilerParams(
            collective_id=0, has_side_effects=True, vmem_limit_bytes=60 * 1024 * 1024
        ),
    )(voltages, feed_gains, grid_slot, transit_start)
    span = NS // owners
    return (
        beam_map.reshape(ch_dev, 4, span),
        transit_snr.reshape(ncal, 4, span),
    )


def solution(mesh):
    in_specs = (
        P("chan", "cyl", None, None, None, "tm"),
        P("chan", "cyl", None, None, None),
        P(),
        P(),
    )
    out_specs = (P("chan", None, ("cyl", "tm")), P(None, None, ("cyl", "tm")))
    return jax.shard_map(
        per_device, mesh=mesh, in_specs=in_specs, out_specs=out_specs, check_vma=False
    )
```

```python
import functools
import math

import jax
import jax.numpy as jnp
from jax import lax
from jax.experimental import pallas as pl
from jax.experimental.pallas import tpu as pltpu
from jax.sharding import PartitionSpec as P

NS = 512
EPSILON = 1e-06
MESH = pl.DeviceIdType.MESH
LANES = 128


def slot_tables(slots, rows, size):
    turns = (slots * rows) & (size - 1)
    eighth = size // 8
    quarter = size // 4
    quadrant = (turns + eighth) // quarter
    rest = turns - quadrant * quarter
    x = rest.astype(jnp.float32) * (2.0 * math.pi / size)
    x2 = x * x
    sine = x * (1.0 + x2 * (-1.0 / 6 + x2 * (1.0 / 120 + x2 * (-1.0 / 5040 + x2 * (1.0 / 362880)))))
    cosine = 1.0 + x2 * (-0.5 + x2 * (1.0 / 24 + x2 * (-1.0 / 720 + x2 * (1.0 / 40320))))
    odd = (quadrant & 1) == 1
    c = jnp.where(odd, sine, cosine)
    s = jnp.where(odd, cosine, sine)
    c = jnp.where((quadrant == 1) | (quadrant == 2), -c, c)
    s = jnp.where((quadrant == 2) | (quadrant == 3), -s, s)
    return c, s


def kernel(
    sizes,
    volt,
    gains,
    slots,
    starts,
    map_out,
    snr_out,
    vbuf,
    gbuf,
    gwide,
    table,
    cal,
    spec,
    acc,
    shapes,
    mom_send,
    mom_recv,
    pool_send,
    pool_recv,
    vs_sem,
    vr_sem,
    gs_sem,
    gr_sem,
    ms_sem,
    mr_sem,
    ps_sem,
    pr_sem,
):
    nchan, ncyl, ntm, ch_dev, fr_dev, pols, feeds, ncal = sizes
    chunks = fr_dev // LANES
    frames = fr_dev * ntm
    window = frames // 2
    channels = ch_dev * nchan
    owners = ncyl * ntm
    my_chan = lax.axis_index("chan")
    me = lax.axis_index("cyl")
    my_tm = lax.axis_index("tm")
    mine = me * ntm + my_tm

    near = me + 1 - 2 * (me % 2)
    middle = (me + 2) % ncyl
    mirror = ncyl - 1 - me
    peers = (near, mirror, middle)

    def owner_device(step):
        target = (mine + step) % owners
        return target, {"cyl": target // ntm, "tm": target % ntm}

    def chan_device(step):
        target = (my_chan + step) % nchan
        return target, {"chan": target}

    barrier = pltpu.get_barrier_semaphore()
    for step in range(1, owners):
        pl.semaphore_signal(barrier, inc=1, device_id=owner_device(step)[1], device_id_type=MESH)
    for step in range(1, nchan):
        pl.semaphore_signal(barrier, inc=1, device_id=chan_device(step)[1], device_id_type=MESH)
    pl.semaphore_wait(barrier, owners - 1 + nchan - 1)

    def gain_copy(j):
        return pltpu.make_async_remote_copy(
            src_ref=gains.at[peers[j], 0],
            dst_ref=gbuf.at[me],
            send_sem=gs_sem.at[j],
            recv_sem=gr_sem.at[me],
            device_id={"cyl": peers[j]},
            device_id_type=MESH,
        )

    def volt_copy(j, k, p, sender):
        return pltpu.make_async_remote_copy(
            src_ref=volt.at[peers[j], 0, p, :, :, pl.ds(k * LANES, LANES)],
            dst_ref=vbuf.at[k, p, sender],
            send_sem=vs_sem.at[j, k, p],
            recv_sem=vr_sem.at[k, p, sender],
            device_id={"cyl": peers[j]},
            device_id_type=MESH,
        )

    def own_volt(k, p):
        return pltpu.make_async_copy(
            volt.at[me, 0, p, :, :, pl.ds(k * LANES, LANES)],
            vbuf.at[k, p, me],
            vr_sem.at[k, p, me],
        )

    own_gain = pltpu.make_async_copy(gains.at[me, 0], gbuf.at[me], gr_sem.at[me])

    for j in range(3):
        gain_copy(j).start()
    own_gain.start()
    pieces = [(k, p) for k in range(chunks) for p in range(pols)]
    for k, p in pieces:
        volt_copy(0, k, p, me).start()
    for k, p in pieces:
        volt_copy(2, k, p, me).start()
        volt_copy(1, k, p, me).start()
    for k, p in pieces:
        own_volt(k, p).start()

    rows_per = 64

    def build(c, carry):
        slot_row = slots[pl.ds(c, 1), :]

        def block(b, inner):
            base = pl.multiple_of(b * rows_per, rows_per)
            row = lax.broadcasted_iota(jnp.int32, (rows_per, feeds), 0) + base
            cosine, sine = slot_tables(slot_row, row, NS)
            factor = 1.0 / math.sqrt(feeds)
            cosine = (cosine * factor).astype(jnp.bfloat16)
            sine = (sine * factor).astype(jnp.bfloat16)
            table[c, pl.ds(base, rows_per), pl.ds(0, feeds)] = cosine
            table[c, pl.ds(base, rows_per), pl.ds(feeds, feeds)] = sine
            low = pl.multiple_of(base + NS, rows_per)
            table[c, pl.ds(low, rows_per), pl.ds(0, feeds)] = -sine
            table[c, pl.ds(low, rows_per), pl.ds(feeds, feeds)] = cosine
            return inner

        return lax.fori_loop(0, NS // rows_per, block, carry)

    lax.fori_loop(0, ncyl, build, 0)

    def template(first, width, k):
        frame = lax.broadcasted_iota(jnp.int32, (8, width), 1) + first
        relative = frame - starts[k]
        inside = (relative >= 0) & (relative < window)
        wave = jnp.sin(math.pi * (relative.astype(jnp.float32) + 0.5) / window)
        return jnp.where(inside, wave * wave, 0.0)

    tsum = []
    tsq = []
    for k in range(ncal):
        whole = template(0, frames, k)[0:1, :]
        tsum.append(jnp.sum(whole, axis=1, keepdims=True))
        tsq.append(jnp.sum(whole * whole, axis=1, keepdims=True))
        own = template(my_tm * fr_dev, fr_dev, k)
        for t in range(chunks):
            shapes[t, k] = own[:, t * LANES : (t + 1) * LANES]

    acc[...] = jnp.zeros_like(acc)

    for j in range(3):
        gain_copy(j).wait_send()
        pltpu.make_async_remote_copy(
            src_ref=gains.at[peers[j], 0],
            dst_ref=gbuf.at[peers[j]],
            send_sem=gs_sem.at[j],
            recv_sem=gr_sem.at[peers[j]],
            device_id={"cyl": peers[j]},
            device_id_type=MESH,
        ).wait_recv()
    own_gain.wait()
    flat = jnp.concatenate([gbuf[c, p] for c in range(ncyl) for p in range(pols)], axis=0)
    tall = flat.T
    for i in range(ncyl * pols * 2):
        gwide[i] = jnp.broadcast_to(tall[:, i : i + 1], (feeds, LANES))

    def chunk_step(k, carry):
        def form(c, p, k):
            i = c * pols + p
            gain_re = gwide[2 * i]
            gain_im = gwide[2 * i + 1]
            volt_re = vbuf[k, p, c, 0].astype(jnp.float32)
            volt_im = vbuf[k, p, c, 1].astype(jnp.float32)
            cal[0:feeds, :] = (gain_re * volt_re - gain_im * volt_im).astype(jnp.bfloat16)
            cal[feeds : 2 * feeds, :] = (gain_re * volt_im + gain_im * volt_re).astype(jnp.bfloat16)
            spec[i] = jnp.dot(table[c], cal[...], preferred_element_type=jnp.float32).astype(
                jnp.bfloat16
            )

        def form_pol(p, inner):
            own_volt(k, p).wait()
            form(me, p, k)
            for j in (0, 2, 1):
                volt_copy(j, k, p, peers[j]).wait_recv()
                form(peers[j], p, k)
            return inner

        lax.fori_loop(0, pols, form_pol, 0)

        rows = 16
        span = NS // owners

        def beams(b, inner):
            base = pl.multiple_of(b * rows, rows)
            owner = b // (span // rows)
            part = (b % (span // rows)) * rows
            power = [None] * 4
            for p in range(pols):
                re = []
                im = []
                for c in range(4):
                    re.append(spec[c * pols + p, pl.ds(base, rows), :].astype(jnp.float32))
                    low = pl.multiple_of(base + NS, rows)
                    im.append(spec[c * pols + p, pl.ds(low, rows), :].astype(jnp.float32))
                re_even, re_odd = re[0] + re[2], re[1] + re[3]
                im_even, im_odd = im[0] + im[2], im[1] + im[3]
                re_alt, im_alt = re[0] - re[2], im[0] - im[2]
                re_skew, im_skew = re[1] - re[3], im[1] - im[3]
                formed = (
                    (re_even + re_odd, im_even + im_odd),
                    (re_alt + im_skew, im_alt - re_skew),
                    (re_even - re_odd, im_even - im_odd),
                    (re_alt - im_skew, im_alt + re_skew),
                )
                for e in range(4):
                    square = formed[e][0] * formed[e][0] + formed[e][1] * formed[e][1]
                    power[e] = square if power[e] is None else power[e] + square
            for e in range(4):
                value = 0.25 * power[e]
                where = pl.ds(pl.multiple_of(e * span + part, rows), rows)
                acc[0, owner, where, :] += value
                acc[1, owner, where, :] += value * value
                for t in range(ncal):
                    shape = shapes[k, t]
                    acc[2 + t, owner, where, :] += value * jnp.concatenate([shape, shape], axis=0)
            return inner

        return lax.fori_loop(0, NS // rows, beams, carry, unroll=2)

    lax.fori_loop(0, chunks, chunk_step, 0)

    lane = lax.broadcasted_iota(jnp.int32, (LANES, LANES), 1)

    def gather(d, carry):
        merged = jnp.zeros((LANES, LANES), jnp.float32)
        for i in range(2 + ncal):
            total = jnp.sum(acc[i, d], axis=1, keepdims=True)
            merged = jnp.where(lane == i, total, merged)
        mom_send[d] = merged.T[0:8, :]
        return carry

    lax.fori_loop(0, owners, gather, 0, unroll=True)

    def moment_copy(step, target, place, device):
        return pltpu.make_async_remote_copy(
            src_ref=mom_send.at[target],
            dst_ref=mom_recv.at[place],
            send_sem=ms_sem.at[step],
            recv_sem=mr_sem.at[place],
            device_id=device,
            device_id_type=MESH,
        )

    for step in range(1, owners):
        target, device = owner_device(step)
        moment_copy(step, target, mine, device).start()
    own_moment = pltpu.make_async_copy(mom_send.at[mine], mom_recv.at[mine], mr_sem.at[mine])
    own_moment.start()
    for step in range(1, owners):
        target, device = owner_device(step)
        moment_copy(step, target, target, device).wait_recv()
    own_moment.wait()

    pooled = jnp.zeros((8, LANES), jnp.float32)
    for z in range(ncyl):
        own = mom_recv[z * ntm]
        for t in range(1, ntm):
            own = own + mom_recv[z * ntm + t]
        map_out[z : z + 1, :] = own[0:1, :] / frames
        pooled = pooled + own
    pool_send[...] = pooled

    def pool_copy(step, place, device):
        return pltpu.make_async_remote_copy(
            src_ref=pool_send,
            dst_ref=pool_recv.at[place],
            send_sem=ps_sem.at[step],
            recv_sem=pr_sem.at[place],
            device_id=device,
            device_id_type=MESH,
        )

    for step in range(1, nchan):
        target, device = chan_device(step)
        pool_copy(step, my_chan, device).start()
    for step in range(1, nchan):
        target, device = chan_device(step)
        pool_copy(step, target, device).wait_recv()
        pooled = pooled + pool_recv[target]

    samples = channels * frames
    zeroth = pooled[0:1, :]
    average = zeroth / samples
    variance = pooled[1:2, :] / samples - average * average
    for k in range(ncal):
        spread = channels * (tsq[k] - tsum[k] * tsum[k] / frames)
        numerator = pooled[2 + k : 3 + k, :] - tsum[k] * zeroth / frames
        snr_out[k : k + 1, :] = numerator / jnp.sqrt(spread * (variance + EPSILON))

    for j in range(3):
        for k, p in pieces:
            volt_copy(j, k, p, me).wait_send()
    for step in range(1, owners):
        target, device = owner_device(step)
        moment_copy(step, target, mine, device).wait_send()
    for step in range(1, nchan):
        target, device = chan_device(step)
        pool_copy(step, my_chan, device).wait_send()


def place_outputs(map_in, snr_in, map_out, snr_out):
    width = map_out.shape[2]
    for e in range(map_out.shape[1]):
        map_out[:, e, :] = map_in[:, e * width : (e + 1) * width]
        snr_out[:, e, :] = snr_in[:, e * width : (e + 1) * width]


def per_device(voltages, feed_gains, grid_slot, transit_start):
    ch_dev, _, pols, _, feeds, fr_dev = voltages.shape
    nchan = lax.axis_size("chan")
    ncyl = lax.axis_size("cyl")
    ntm = lax.axis_size("tm")
    ncal = transit_start.shape[0]
    assert ncyl == 4 and ch_dev == ncyl
    chunks = fr_dev // LANES
    owners = ncyl * ntm
    sizes = (nchan, ncyl, ntm, ch_dev, fr_dev, pols, feeds, ncal)
    dma = pltpu.SemaphoreType.DMA
    f32 = jnp.float32
    bf16 = jnp.bfloat16
    beam_map, transit_snr = pl.pallas_call(
        functools.partial(kernel, sizes),
        out_shape=(
            jax.ShapeDtypeStruct((ch_dev, LANES), f32),
            jax.ShapeDtypeStruct((ncal, LANES), f32),
        ),
        in_specs=[
            pl.BlockSpec(memory_space=pl.ANY),
            pl.BlockSpec(memory_space=pl.ANY),
            pl.BlockSpec(memory_space=pltpu.VMEM),
            pl.BlockSpec(memory_space=pltpu.SMEM),
        ],
        out_specs=(
            pl.BlockSpec(memory_space=pltpu.VMEM),
            pl.BlockSpec(memory_space=pltpu.VMEM),
        ),
        scratch_shapes=[
            pltpu.VMEM((chunks, pols, ncyl, 2, feeds, LANES), bf16),
            pltpu.VMEM((ncyl, pols, 2, feeds), f32),
            pltpu.VMEM((ncyl * pols * 2, feeds, LANES), f32),
            pltpu.VMEM((ncyl, 2 * NS, 2 * feeds), bf16),
            pltpu.VMEM((2 * feeds, LANES), bf16),
            pltpu.VMEM((ncyl * pols, 2 * NS, LANES), bf16),
            pltpu.VMEM((2 + ncal, owners, 4 * NS // owners, LANES), f32),
            pltpu.VMEM((chunks, ncal, 8, LANES), f32),
            pltpu.VMEM((owners, 8, LANES), f32),
            pltpu.VMEM((owners, 8, LANES), f32),
            pltpu.VMEM((8, LANES), f32),
            pltpu.VMEM((nchan, 8, LANES), f32),
            dma((3, chunks, pols)),
            dma((chunks, pols, ncyl)),
            dma((3,)),
            dma((ncyl,)),
            dma((owners,)),
            dma((owners,)),
            dma((nchan,)),
            dma((nchan,)),
        ],
        compiler_params=pltpu.CompilerParams(
            collective_id=0, has_side_effects=True, vmem_limit_bytes=60 * 1024 * 1024
        ),
    )(voltages, feed_gains, grid_slot, transit_start)
    span = NS // owners
    vmem = pl.BlockSpec(memory_space=pltpu.VMEM)
    return pl.pallas_call(
        place_outputs,
        out_shape=(
            jax.ShapeDtypeStruct((ch_dev, 4, span), f32),
            jax.ShapeDtypeStruct((ncal, 4, span), f32),
        ),
        in_specs=[vmem, vmem],
        out_specs=(vmem, vmem),
    )(beam_map, transit_snr)


def solution(mesh):
    in_specs = (
        P("chan", "cyl", None, None, None, "tm"),
        P("chan", "cyl", None, None, None),
        P(),
        P(),
    )
    out_specs = (P("chan", None, ("cyl", "tm")), P(None, None, ("cyl", "tm")))
    return jax.shard_map(
        per_device, mesh=mesh, in_specs=in_specs, out_specs=out_specs, check_vma=False
    )
```

```python
import functools
import math

import jax
import jax.numpy as jnp
from jax import lax
from jax.experimental import pallas as pl
from jax.experimental.pallas import tpu as pltpu
from jax.sharding import PartitionSpec as P

NS = 512
EPSILON = 1e-06
MESH = pl.DeviceIdType.MESH
LANES = 128


def slot_tables(slots, rows, size):
    turns = (slots * rows) & (size - 1)
    eighth = size // 8
    quarter = size // 4
    quadrant = (turns + eighth) // quarter
    rest = turns - quadrant * quarter
    x = rest.astype(jnp.float32) * (2.0 * math.pi / size)
    x2 = x * x
    sine = x * (1.0 + x2 * (-1.0 / 6 + x2 * (1.0 / 120 + x2 * (-1.0 / 5040 + x2 * (1.0 / 362880)))))
    cosine = 1.0 + x2 * (-0.5 + x2 * (1.0 / 24 + x2 * (-1.0 / 720 + x2 * (1.0 / 40320))))
    odd = (quadrant & 1) == 1
    c = jnp.where(odd, sine, cosine)
    s = jnp.where(odd, cosine, sine)
    c = jnp.where((quadrant == 1) | (quadrant == 2), -c, c)
    s = jnp.where((quadrant == 2) | (quadrant == 3), -s, s)
    return c, s


def kernel(
    sizes,
    volt,
    gains,
    slots,
    starts,
    map_out,
    snr_out,
    vbuf,
    gbuf,
    gwide,
    table,
    cal,
    spec,
    acc,
    shapes,
    mom_send,
    mom_recv,
    pool_send,
    pool_recv,
    vs_sem,
    vr_sem,
    gs_sem,
    gr_sem,
    ms_sem,
    mr_sem,
    ps_sem,
    pr_sem,
    hop_sem,
):
    nchan, ncyl, ntm, ch_dev, fr_dev, pols, feeds, ncal = sizes
    chunks = fr_dev // LANES
    frames = fr_dev * ntm
    window = frames // 2
    channels = ch_dev * nchan
    owners = ncyl * ntm
    my_chan = lax.axis_index("chan")
    me = lax.axis_index("cyl")
    my_tm = lax.axis_index("tm")
    mine = me * ntm + my_tm

    near = me + 1 - 2 * (me % 2)
    middle = (me + 2) % ncyl
    mirror = ncyl - 1 - me
    peers = (near, mirror, middle)

    others = []
    for z in (mirror, middle, near, me):
        for dt in range(1 if z is me else 0, ntm):
            t = (my_tm + dt) % ntm
            others.append((z * ntm + t, {"cyl": z, "tm": t}))

    def chan_device(step):
        target = (my_chan + step) % nchan
        return target, {"chan": target}

    inner = (me == 1) | (me == 2)
    inward = jnp.where(me < 2, me + 1, me - 1)

    barrier = pltpu.get_barrier_semaphore()
    pl.semaphore_signal(barrier, inc=1, device_id={"cyl": inward}, device_id_type=MESH)

    @pl.when(inner)
    def _():
        pl.semaphore_signal(barrier, inc=1, device_id={"cyl": near}, device_id_type=MESH)

    for step in range(1, ntm):
        pl.semaphore_signal(
            barrier, inc=1, device_id={"tm": (my_tm + step) % ntm}, device_id_type=MESH
        )
    for step in range(1, nchan):
        pl.semaphore_signal(barrier, inc=1, device_id=chan_device(step)[1], device_id_type=MESH)
    pl.semaphore_wait(barrier, jnp.where(inner, 2, 1) + ntm - 1 + nchan - 1)

    def gain_copy(j):
        return pltpu.make_async_remote_copy(
            src_ref=gains.at[peers[j], 0],
            dst_ref=gbuf.at[me],
            send_sem=gs_sem.at[j],
            recv_sem=gr_sem.at[me],
            device_id={"cyl": peers[j]},
            device_id_type=MESH,
        )

    def volt_copy(j, k, p, sender):
        return pltpu.make_async_remote_copy(
            src_ref=volt.at[peers[j], 0, p, :, :, pl.ds(k * LANES, LANES)],
            dst_ref=vbuf.at[k, p, sender],
            send_sem=vs_sem.at[j, k, p],
            recv_sem=vr_sem.at[k, p, sender],
            device_id={"cyl": peers[j]},
            device_id_type=MESH,
        )

    def own_volt(k, p):
        return pltpu.make_async_copy(
            volt.at[me, 0, p, :, :, pl.ds(k * LANES, LANES)],
            vbuf.at[k, p, me],
            vr_sem.at[k, p, me],
        )

    own_gain = pltpu.make_async_copy(gains.at[me, 0], gbuf.at[me], gr_sem.at[me])

    pieces = [(k, p) for k in range(chunks) for p in range(pols)]
    gain_copy(0).start()
    own_gain.start()
    for k, p in pieces:
        volt_copy(0, k, p, me).start()

    @pl.when(inner)
    def _():
        for p in range(pols):
            volt_copy(1, 0, p, me).start()

    pl.semaphore_signal(hop_sem.at[0], inc=1, device_id={"cyl": inward}, device_id_type=MESH)

    @pl.when(inner)
    def _():
        pl.semaphore_signal(hop_sem.at[0], inc=1, device_id={"cyl": near}, device_id_type=MESH)
        pl.semaphore_wait(hop_sem.at[0], 2)
        pl.semaphore_signal(hop_sem.at[1], inc=1, device_id={"cyl": near}, device_id_type=MESH)

    @pl.when(jnp.logical_not(inner))
    def _():
        pl.semaphore_wait(hop_sem.at[0], 1)
        pl.semaphore_wait(hop_sem.at[1], 1)

    gain_copy(1).start()
    gain_copy(2).start()

    @pl.when(jnp.logical_not(inner))
    def _():
        for p in range(pols):
            volt_copy(2, 0, p, me).start()
            volt_copy(1, 0, p, me).start()

    @pl.when(inner)
    def _():
        for p in range(pols):
            volt_copy(2, 0, p, me).start()

    for k, p in pieces[pols:]:
        volt_copy(2, k, p, me).start()
        volt_copy(1, k, p, me).start()
    for k, p in pieces:
        own_volt(k, p).start()

    rows_per = 64

    def build(c, carry):
        slot_row = slots[pl.ds(c, 1), :]

        def block(b, inner):
            base = pl.multiple_of(b * rows_per, rows_per)
            row = lax.broadcasted_iota(jnp.int32, (rows_per, feeds), 0) + base
            cosine, sine = slot_tables(slot_row, row, NS)
            factor = 1.0 / math.sqrt(feeds)
            cosine = (cosine * factor).astype(jnp.bfloat16)
            sine = (sine * factor).astype(jnp.bfloat16)
            table[c, pl.ds(base, rows_per), pl.ds(0, feeds)] = cosine
            table[c, pl.ds(base, rows_per), pl.ds(feeds, feeds)] = sine
            low = pl.multiple_of(base + NS, rows_per)
            table[c, pl.ds(low, rows_per), pl.ds(0, feeds)] = -sine
            table[c, pl.ds(low, rows_per), pl.ds(feeds, feeds)] = cosine
            return inner

        return lax.fori_loop(0, NS // rows_per, block, carry)

    lax.fori_loop(0, ncyl, build, 0)

    def template(first, width, k):
        frame = lax.broadcasted_iota(jnp.int32, (8, width), 1) + first
        relative = frame - starts[k]
        inside = (relative >= 0) & (relative < window)
        wave = jnp.sin(math.pi * (relative.astype(jnp.float32) + 0.5) / window)
        return jnp.where(inside, wave * wave, 0.0)

    tsum = []
    tsq = []
    for k in range(ncal):
        whole = template(0, frames, k)[0:1, :]
        tsum.append(jnp.sum(whole, axis=1, keepdims=True))
        tsq.append(jnp.sum(whole * whole, axis=1, keepdims=True))
        own = template(my_tm * fr_dev, fr_dev, k)
        for t in range(chunks):
            shapes[t, k] = own[:, t * LANES : (t + 1) * LANES]

    acc[...] = jnp.zeros_like(acc)

    for j in range(3):
        gain_copy(j).wait_send()
        pltpu.make_async_remote_copy(
            src_ref=gains.at[peers[j], 0],
            dst_ref=gbuf.at[peers[j]],
            send_sem=gs_sem.at[j],
            recv_sem=gr_sem.at[peers[j]],
            device_id={"cyl": peers[j]},
            device_id_type=MESH,
        ).wait_recv()
    own_gain.wait()
    flat = jnp.concatenate([gbuf[c, p] for c in range(ncyl) for p in range(pols)], axis=0)
    tall = flat.T
    for i in range(ncyl * pols * 2):
        gwide[i] = jnp.broadcast_to(tall[:, i : i + 1], (feeds, LANES))

    def chunk_step(k, carry):
        def form(c, p, k):
            i = c * pols + p
            gain_re = gwide[2 * i]
            gain_im = gwide[2 * i + 1]
            volt_re = vbuf[k, p, c, 0].astype(jnp.float32)
            volt_im = vbuf[k, p, c, 1].astype(jnp.float32)
            cal[0:feeds, :] = (gain_re * volt_re - gain_im * volt_im).astype(jnp.bfloat16)
            cal[feeds : 2 * feeds, :] = (gain_re * volt_im + gain_im * volt_re).astype(jnp.bfloat16)
            spec[i] = jnp.dot(table[c], cal[...], preferred_element_type=jnp.float32).astype(
                jnp.bfloat16
            )

        def form_pol(p, inner):
            own_volt(k, p).wait()
            form(me, p, k)
            for j in (0, 2, 1):
                volt_copy(j, k, p, peers[j]).wait_recv()
                form(peers[j], p, k)
            return inner

        lax.fori_loop(0, pols, form_pol, 0)

        rows = 16
        span = NS // owners

        def beams(b, inner):
            base = pl.multiple_of(b * rows, rows)
            owner = b // (span // rows)
            part = (b % (span // rows)) * rows
            power = [None] * 4
            for p in range(pols):
                re = []
                im = []
                for c in range(4):
                    re.append(spec[c * pols + p, pl.ds(base, rows), :].astype(jnp.float32))
                    low = pl.multiple_of(base + NS, rows)
                    im.append(spec[c * pols + p, pl.ds(low, rows), :].astype(jnp.float32))
                re_even, re_odd = re[0] + re[2], re[1] + re[3]
                im_even, im_odd = im[0] + im[2], im[1] + im[3]
                re_alt, im_alt = re[0] - re[2], im[0] - im[2]
                re_skew, im_skew = re[1] - re[3], im[1] - im[3]
                formed = (
                    (re_even + re_odd, im_even + im_odd),
                    (re_alt + im_skew, im_alt - re_skew),
                    (re_even - re_odd, im_even - im_odd),
                    (re_alt - im_skew, im_alt + re_skew),
                )
                for e in range(4):
                    square = formed[e][0] * formed[e][0] + formed[e][1] * formed[e][1]
                    power[e] = square if power[e] is None else power[e] + square
            for e in range(4):
                value = 0.25 * power[e]
                where = pl.ds(pl.multiple_of(e * span + part, rows), rows)
                acc[0, owner, where, :] += value
                acc[1, owner, where, :] += value * value
                for t in range(ncal):
                    shape = shapes[k, t]
                    acc[2 + t, owner, where, :] += value * jnp.concatenate([shape, shape], axis=0)
            return inner

        return lax.fori_loop(0, NS // rows, beams, carry, unroll=2)

    lax.fori_loop(0, chunks, chunk_step, 0)

    lane = lax.broadcasted_iota(jnp.int32, (LANES, LANES), 1)

    def gather(d, carry):
        merged = jnp.zeros((LANES, LANES), jnp.float32)
        for i in range(2 + ncal):
            total = jnp.sum(acc[i, d], axis=1, keepdims=True)
            merged = jnp.where(lane == i, total, merged)
        mom_send[d] = merged.T[0:8, :]
        return carry

    lax.fori_loop(0, owners, gather, 0, unroll=True)

    def moment_copy(step, target, place, device):
        return pltpu.make_async_remote_copy(
            src_ref=mom_send.at[target],
            dst_ref=mom_recv.at[place],
            send_sem=ms_sem.at[step],
            recv_sem=mr_sem.at[place],
            device_id=device,
            device_id_type=MESH,
        )

    for step, (target, device) in enumerate(others):
        moment_copy(step, target, mine, device).start()
    own_moment = pltpu.make_async_copy(mom_send.at[mine], mom_recv.at[mine], mr_sem.at[mine])
    own_moment.start()
    for step, (target, device) in enumerate(others):
        moment_copy(step, target, target, device).wait_recv()
    own_moment.wait()

    pooled = jnp.zeros((8, LANES), jnp.float32)
    for z in range(ncyl):
        own = mom_recv[z * ntm]
        for t in range(1, ntm):
            own = own + mom_recv[z * ntm + t]
        map_out[z : z + 1, :] = own[0:1, :] / frames
        pooled = pooled + own
    pool_send[...] = pooled

    def pool_copy(step, place, device):
        return pltpu.make_async_remote_copy(
            src_ref=pool_send,
            dst_ref=pool_recv.at[place],
            send_sem=ps_sem.at[step],
            recv_sem=pr_sem.at[place],
            device_id=device,
            device_id_type=MESH,
        )

    for step in range(1, nchan):
        target, device = chan_device(step)
        pool_copy(step, my_chan, device).start()
    for step in range(1, nchan):
        target, device = chan_device(step)
        pool_copy(step, target, device).wait_recv()
        pooled = pooled + pool_recv[target]

    samples = channels * frames
    zeroth = pooled[0:1, :]
    average = zeroth / samples
    variance = pooled[1:2, :] / samples - average * average
    for k in range(ncal):
        spread = channels * (tsq[k] - tsum[k] * tsum[k] / frames)
        numerator = pooled[2 + k : 3 + k, :] - tsum[k] * zeroth / frames
        snr_out[k : k + 1, :] = numerator / jnp.sqrt(spread * (variance + EPSILON))

    for j in range(3):
        for k, p in pieces:
            volt_copy(j, k, p, me).wait_send()
    for step, (target, device) in enumerate(others):
        moment_copy(step, target, mine, device).wait_send()
    for step in range(1, nchan):
        target, device = chan_device(step)
        pool_copy(step, my_chan, device).wait_send()


def place_outputs(map_in, snr_in, map_out, snr_out):
    width = map_out.shape[2]
    for e in range(map_out.shape[1]):
        map_out[:, e, :] = map_in[:, e * width : (e + 1) * width]
        snr_out[:, e, :] = snr_in[:, e * width : (e + 1) * width]


def per_device(voltages, feed_gains, grid_slot, transit_start):
    ch_dev, _, pols, _, feeds, fr_dev = voltages.shape
    nchan = lax.axis_size("chan")
    ncyl = lax.axis_size("cyl")
    ntm = lax.axis_size("tm")
    ncal = transit_start.shape[0]
    assert ncyl == 4 and ch_dev == ncyl
    chunks = fr_dev // LANES
    owners = ncyl * ntm
    sizes = (nchan, ncyl, ntm, ch_dev, fr_dev, pols, feeds, ncal)
    dma = pltpu.SemaphoreType.DMA
    f32 = jnp.float32
    bf16 = jnp.bfloat16
    beam_map, transit_snr = pl.pallas_call(
        functools.partial(kernel, sizes),
        out_shape=(
            jax.ShapeDtypeStruct((ch_dev, LANES), f32),
            jax.ShapeDtypeStruct((ncal, LANES), f32),
        ),
        in_specs=[
            pl.BlockSpec(memory_space=pl.ANY),
            pl.BlockSpec(memory_space=pl.ANY),
            pl.BlockSpec(memory_space=pltpu.VMEM),
            pl.BlockSpec(memory_space=pltpu.SMEM),
        ],
        out_specs=(
            pl.BlockSpec(memory_space=pltpu.VMEM),
            pl.BlockSpec(memory_space=pltpu.VMEM),
        ),
        scratch_shapes=[
            pltpu.VMEM((chunks, pols, ncyl, 2, feeds, LANES), bf16),
            pltpu.VMEM((ncyl, pols, 2, feeds), f32),
            pltpu.VMEM((ncyl * pols * 2, feeds, LANES), f32),
            pltpu.VMEM((ncyl, 2 * NS, 2 * feeds), bf16),
            pltpu.VMEM((2 * feeds, LANES), bf16),
            pltpu.VMEM((ncyl * pols, 2 * NS, LANES), bf16),
            pltpu.VMEM((2 + ncal, owners, 4 * NS // owners, LANES), f32),
            pltpu.VMEM((chunks, ncal, 8, LANES), f32),
            pltpu.VMEM((owners, 8, LANES), f32),
            pltpu.VMEM((owners, 8, LANES), f32),
            pltpu.VMEM((8, LANES), f32),
            pltpu.VMEM((nchan, 8, LANES), f32),
            dma((3, chunks, pols)),
            dma((chunks, pols, ncyl)),
            dma((3,)),
            dma((ncyl,)),
            dma((owners,)),
            dma((owners,)),
            dma((nchan,)),
            dma((nchan,)),
            pltpu.SemaphoreType.REGULAR((2,)),
        ],
        compiler_params=pltpu.CompilerParams(
            collective_id=0, has_side_effects=True, vmem_limit_bytes=60 * 1024 * 1024
        ),
    )(voltages, feed_gains, grid_slot, transit_start)
    span = NS // owners
    vmem = pl.BlockSpec(memory_space=pltpu.VMEM)
    return pl.pallas_call(
        place_outputs,
        out_shape=(
            jax.ShapeDtypeStruct((ch_dev, 4, span), f32),
            jax.ShapeDtypeStruct((ncal, 4, span), f32),
        ),
        in_specs=[vmem, vmem],
        out_specs=(vmem, vmem),
    )(beam_map, transit_snr)


def solution(mesh):
    in_specs = (
        P("chan", "cyl", None, None, None, "tm"),
        P("chan", "cyl", None, None, None),
        P(),
        P(),
    )
    out_specs = (P("chan", None, ("cyl", "tm")), P(None, None, ("cyl", "tm")))
    return jax.shard_map(
        per_device, mesh=mesh, in_specs=in_specs, out_specs=out_specs, check_vma=False
    )
```

```python
import functools
import math

import jax
import jax.numpy as jnp
from jax import lax
from jax.experimental import pallas as pl
from jax.experimental.pallas import tpu as pltpu
from jax.sharding import PartitionSpec as P

NS = 512
EPSILON = 1e-06
MESH = pl.DeviceIdType.MESH
LANES = 128


def slot_tables(slots, rows, size):
    turns = (slots * rows) & (size - 1)
    eighth = size // 8
    quarter = size // 4
    quadrant = (turns + eighth) // quarter
    rest = turns - quadrant * quarter
    x = rest.astype(jnp.float32) * (2.0 * math.pi / size)
    x2 = x * x
    sine = x * (1.0 + x2 * (-1.0 / 6 + x2 * (1.0 / 120 + x2 * (-1.0 / 5040 + x2 * (1.0 / 362880)))))
    cosine = 1.0 + x2 * (-0.5 + x2 * (1.0 / 24 + x2 * (-1.0 / 720 + x2 * (1.0 / 40320))))
    odd = (quadrant & 1) == 1
    c = jnp.where(odd, sine, cosine)
    s = jnp.where(odd, cosine, sine)
    c = jnp.where((quadrant == 1) | (quadrant == 2), -c, c)
    s = jnp.where((quadrant == 2) | (quadrant == 3), -s, s)
    return c, s


def kernel(
    sizes,
    volt,
    gains,
    slots,
    starts,
    map_out,
    snr_out,
    vbuf,
    gbuf,
    gwide,
    table,
    cal,
    spec,
    acc,
    shapes,
    mom_send,
    mom_recv,
    pool_send,
    pool_recv,
    vs_sem,
    vr_sem,
    gs_sem,
    gr_sem,
    ms_sem,
    mr_sem,
    ps_sem,
    pr_sem,
    hop_sem,
):
    nchan, ncyl, ntm, ch_dev, fr_dev, pols, feeds, ncal = sizes
    chunks = fr_dev // LANES
    frames = fr_dev * ntm
    window = frames // 2
    channels = ch_dev * nchan
    owners = ncyl * ntm
    my_chan = lax.axis_index("chan")
    me = lax.axis_index("cyl")
    my_tm = lax.axis_index("tm")
    mine = me * ntm + my_tm

    near = me + 1 - 2 * (me % 2)
    middle = (me + 2) % ncyl
    mirror = ncyl - 1 - me
    peers = (near, mirror, middle)

    others = []
    for z in (mirror, middle, near, me):
        for dt in range(1 if z is me else 0, ntm):
            t = (my_tm + dt) % ntm
            others.append((z * ntm + t, {"cyl": z, "tm": t}))

    def chan_device(step):
        target = (my_chan + step) % nchan
        return target, {"chan": target}

    inner = (me == 1) | (me == 2)
    inward = jnp.where(me < 2, me + 1, me - 1)

    barrier = pltpu.get_barrier_semaphore()
    pl.semaphore_signal(barrier, inc=1, device_id={"cyl": inward}, device_id_type=MESH)

    @pl.when(inner)
    def _():
        pl.semaphore_signal(barrier, inc=1, device_id={"cyl": near}, device_id_type=MESH)

    for step in range(1, ntm):
        pl.semaphore_signal(
            barrier, inc=1, device_id={"tm": (my_tm + step) % ntm}, device_id_type=MESH
        )
    for step in range(1, nchan):
        pl.semaphore_signal(barrier, inc=1, device_id=chan_device(step)[1], device_id_type=MESH)
    pl.semaphore_wait(barrier, jnp.where(inner, 2, 1) + ntm - 1 + nchan - 1)

    def gain_copy(j):
        return pltpu.make_async_remote_copy(
            src_ref=gains.at[peers[j], 0],
            dst_ref=gbuf.at[me],
            send_sem=gs_sem.at[j],
            recv_sem=gr_sem.at[me],
            device_id={"cyl": peers[j]},
            device_id_type=MESH,
        )

    def volt_copy(j, k, p, sender):
        return pltpu.make_async_remote_copy(
            src_ref=volt.at[peers[j], 0, p, :, :, pl.ds(k * LANES, LANES)],
            dst_ref=vbuf.at[k, p, sender],
            send_sem=vs_sem.at[j, k, p],
            recv_sem=vr_sem.at[k, p, sender],
            device_id={"cyl": peers[j]},
            device_id_type=MESH,
        )

    def own_volt(k, p):
        return pltpu.make_async_copy(
            volt.at[me, 0, p, :, :, pl.ds(k * LANES, LANES)],
            vbuf.at[k, p, me],
            vr_sem.at[k, p, me],
        )

    own_gain = pltpu.make_async_copy(gains.at[me, 0], gbuf.at[me], gr_sem.at[me])

    pieces = [(k, p) for k in range(chunks) for p in range(pols)]
    gain_copy(0).start()
    own_gain.start()
    for k, p in pieces:
        volt_copy(0, k, p, me).start()

    @pl.when(inner)
    def _():
        for p in range(pols):
            volt_copy(1, 0, p, me).start()

    pl.semaphore_signal(hop_sem.at[0], inc=1, device_id={"cyl": inward}, device_id_type=MESH)

    @pl.when(inner)
    def _():
        pl.semaphore_signal(hop_sem.at[0], inc=1, device_id={"cyl": near}, device_id_type=MESH)
        pl.semaphore_wait(hop_sem.at[0], 2)
        pl.semaphore_signal(hop_sem.at[1], inc=1, device_id={"cyl": near}, device_id_type=MESH)

    @pl.when(jnp.logical_not(inner))
    def _():
        pl.semaphore_wait(hop_sem.at[0], 1)
        pl.semaphore_wait(hop_sem.at[1], 1)

    gain_copy(1).start()
    gain_copy(2).start()

    @pl.when(jnp.logical_not(inner))
    def _():
        for p in range(pols):
            volt_copy(2, 0, p, me).start()
            volt_copy(1, 0, p, me).start()

    @pl.when(inner)
    def _():
        for p in range(pols):
            volt_copy(2, 0, p, me).start()

    for k, p in pieces[pols:]:
        volt_copy(2, k, p, me).start()
        volt_copy(1, k, p, me).start()
    for k, p in pieces:
        own_volt(k, p).start()

    rows_per = 64

    def build(c, carry):
        slot_row = slots[pl.ds(c, 1), :]

        def block(b, inner):
            base = pl.multiple_of(b * rows_per, rows_per)
            row = lax.broadcasted_iota(jnp.int32, (rows_per, feeds), 0) + base
            cosine, sine = slot_tables(slot_row, row, NS)
            factor = 1.0 / math.sqrt(feeds)
            cosine = (cosine * factor).astype(jnp.bfloat16)
            sine = (sine * factor).astype(jnp.bfloat16)
            table[c, pl.ds(base, rows_per), pl.ds(0, feeds)] = cosine
            table[c, pl.ds(base, rows_per), pl.ds(feeds, feeds)] = sine
            low = pl.multiple_of(base + NS, rows_per)
            table[c, pl.ds(low, rows_per), pl.ds(0, feeds)] = -sine
            table[c, pl.ds(low, rows_per), pl.ds(feeds, feeds)] = cosine
            return inner

        return lax.fori_loop(0, NS // rows_per, block, carry)

    lax.fori_loop(0, ncyl, build, 0)

    def template(first, width, k):
        frame = lax.broadcasted_iota(jnp.int32, (8, width), 1) + first
        relative = frame - starts[k]
        inside = (relative >= 0) & (relative < window)
        wave = jnp.sin(math.pi * (relative.astype(jnp.float32) + 0.5) / window)
        return jnp.where(inside, wave * wave, 0.0)

    tsum = []
    tsq = []
    for k in range(ncal):
        whole = template(0, frames, k)[0:1, :]
        tsum.append(jnp.sum(whole, axis=1, keepdims=True))
        tsq.append(jnp.sum(whole * whole, axis=1, keepdims=True))
        own = template(my_tm * fr_dev, fr_dev, k)
        for t in range(chunks):
            shapes[t, k] = own[:, t * LANES : (t + 1) * LANES]

    acc[...] = jnp.zeros_like(acc)

    for j in range(3):
        gain_copy(j).wait_send()
        pltpu.make_async_remote_copy(
            src_ref=gains.at[peers[j], 0],
            dst_ref=gbuf.at[peers[j]],
            send_sem=gs_sem.at[j],
            recv_sem=gr_sem.at[peers[j]],
            device_id={"cyl": peers[j]},
            device_id_type=MESH,
        ).wait_recv()
    own_gain.wait()
    flat = jnp.concatenate([gbuf[c, p] for c in range(ncyl) for p in range(pols)], axis=0)
    tall = flat.T
    for i in range(ncyl * pols * 2):
        gwide[i] = jnp.broadcast_to(tall[:, i : i + 1], (feeds, LANES))

    def chunk_step(k, carry):
        def form(c, p, k):
            i = c * pols + p
            gain_re = gwide[2 * i]
            gain_im = gwide[2 * i + 1]
            volt_re = vbuf[k, p, c, 0].astype(jnp.float32)
            volt_im = vbuf[k, p, c, 1].astype(jnp.float32)
            cal[0:feeds, :] = (gain_re * volt_re - gain_im * volt_im).astype(jnp.bfloat16)
            cal[feeds : 2 * feeds, :] = (gain_re * volt_im + gain_im * volt_re).astype(jnp.bfloat16)
            spec[i] = jnp.dot(table[c], cal[...], preferred_element_type=jnp.float32).astype(
                jnp.bfloat16
            )

        def form_pol(p, inner):
            own_volt(k, p).wait()
            form(me, p, k)
            for j in (0, 2, 1):
                volt_copy(j, k, p, peers[j]).wait_recv()
                form(peers[j], p, k)
            return inner

        lax.fori_loop(0, pols, form_pol, 0)

        rows = 16
        span = NS // owners

        def beams(b, inner):
            base = pl.multiple_of(b * rows, rows)
            owner = b // (span // rows)
            part = (b % (span // rows)) * rows
            power = [None] * 4
            for p in range(pols):
                re = []
                im = []
                for c in range(4):
                    re.append(spec[c * pols + p, pl.ds(base, rows), :].astype(jnp.float32))
                    low = pl.multiple_of(base + NS, rows)
                    im.append(spec[c * pols + p, pl.ds(low, rows), :].astype(jnp.float32))
                re_even, re_odd = re[0] + re[2], re[1] + re[3]
                im_even, im_odd = im[0] + im[2], im[1] + im[3]
                re_alt, im_alt = re[0] - re[2], im[0] - im[2]
                re_skew, im_skew = re[1] - re[3], im[1] - im[3]
                formed = (
                    (re_even + re_odd, im_even + im_odd),
                    (re_alt + im_skew, im_alt - re_skew),
                    (re_even - re_odd, im_even - im_odd),
                    (re_alt - im_skew, im_alt + re_skew),
                )
                for e in range(4):
                    square = formed[e][0] * formed[e][0] + formed[e][1] * formed[e][1]
                    power[e] = square if power[e] is None else power[e] + square
            for e in range(4):
                value = 0.25 * power[e]
                where = pl.ds(pl.multiple_of(e * span + part, rows), rows)
                acc[0, owner, where, :] += value
                acc[1, owner, where, :] += value * value
                for t in range(ncal):
                    shape = shapes[k, t]
                    acc[2 + t, owner, where, :] += value * jnp.concatenate([shape, shape], axis=0)
            return inner

        return lax.fori_loop(0, NS // rows, beams, carry, unroll=2)

    lax.fori_loop(0, chunks, chunk_step, 0)

    lane = lax.broadcasted_iota(jnp.int32, (LANES, LANES), 1)

    def gather(d, carry):
        merged = jnp.zeros((LANES, LANES), jnp.float32)
        for i in range(2 + ncal):
            total = jnp.sum(acc[i, d], axis=1, keepdims=True)
            merged = jnp.where(lane == i, total, merged)
        mom_send[d] = merged.T[0:8, :]
        return carry

    lax.fori_loop(0, owners, gather, 0, unroll=True)

    def moment_copy(step, target, place, device):
        return pltpu.make_async_remote_copy(
            src_ref=mom_send.at[target],
            dst_ref=mom_recv.at[place],
            send_sem=ms_sem.at[step],
            recv_sem=mr_sem.at[place],
            device_id=device,
            device_id_type=MESH,
        )

    for step, (target, device) in enumerate(others):
        moment_copy(step, target, mine, device).start()
    own_moment = pltpu.make_async_copy(mom_send.at[mine], mom_recv.at[mine], mr_sem.at[mine])
    own_moment.start()
    for step, (target, device) in enumerate(others):
        moment_copy(step, target, target, device).wait_recv()
    own_moment.wait()

    sums = []
    pooled = jnp.zeros((8, LANES), jnp.float32)
    for z in range(ncyl):
        own = mom_recv[z * ntm]
        for t in range(1, ntm):
            own = own + mom_recv[z * ntm + t]
        sums.append(own)
        pooled = pooled + own
    pool_send[...] = pooled

    def pool_copy(step, place, device):
        return pltpu.make_async_remote_copy(
            src_ref=pool_send,
            dst_ref=pool_recv.at[place],
            send_sem=ps_sem.at[step],
            recv_sem=pr_sem.at[place],
            device_id=device,
            device_id_type=MESH,
        )

    for step in range(1, nchan):
        target, device = chan_device(step)
        pool_copy(step, my_chan, device).start()
    for z in range(ncyl):
        map_out[z : z + 1, :] = sums[z][0:1, :] / frames
    for j in range(3):
        for k, p in pieces:
            volt_copy(j, k, p, me).wait_send()
    for step, (target, device) in enumerate(others):
        moment_copy(step, target, mine, device).wait_send()
    for step in range(1, nchan):
        target, device = chan_device(step)
        pool_copy(step, target, device).wait_recv()
        pooled = pooled + pool_recv[target]

    samples = channels * frames
    zeroth = pooled[0:1, :]
    average = zeroth / samples
    variance = pooled[1:2, :] / samples - average * average
    for k in range(ncal):
        spread = channels * (tsq[k] - tsum[k] * tsum[k] / frames)
        numerator = pooled[2 + k : 3 + k, :] - tsum[k] * zeroth / frames
        snr_out[k : k + 1, :] = numerator / jnp.sqrt(spread * (variance + EPSILON))

    for step in range(1, nchan):
        target, device = chan_device(step)
        pool_copy(step, my_chan, device).wait_send()


def place_outputs(map_in, snr_in, map_out, snr_out):
    width = map_out.shape[2]
    for e in range(map_out.shape[1]):
        map_out[:, e, :] = map_in[:, e * width : (e + 1) * width]
        snr_out[:, e, :] = snr_in[:, e * width : (e + 1) * width]


def per_device(voltages, feed_gains, grid_slot, transit_start):
    ch_dev, _, pols, _, feeds, fr_dev = voltages.shape
    nchan = lax.axis_size("chan")
    ncyl = lax.axis_size("cyl")
    ntm = lax.axis_size("tm")
    ncal = transit_start.shape[0]
    assert ncyl == 4 and ch_dev == ncyl
    chunks = fr_dev // LANES
    owners = ncyl * ntm
    sizes = (nchan, ncyl, ntm, ch_dev, fr_dev, pols, feeds, ncal)
    dma = pltpu.SemaphoreType.DMA
    f32 = jnp.float32
    bf16 = jnp.bfloat16
    beam_map, transit_snr = pl.pallas_call(
        functools.partial(kernel, sizes),
        out_shape=(
            jax.ShapeDtypeStruct((ch_dev, LANES), f32),
            jax.ShapeDtypeStruct((ncal, LANES), f32),
        ),
        in_specs=[
            pl.BlockSpec(memory_space=pl.ANY),
            pl.BlockSpec(memory_space=pl.ANY),
            pl.BlockSpec(memory_space=pltpu.VMEM),
            pl.BlockSpec(memory_space=pltpu.SMEM),
        ],
        out_specs=(
            pl.BlockSpec(memory_space=pltpu.VMEM),
            pl.BlockSpec(memory_space=pltpu.VMEM),
        ),
        scratch_shapes=[
            pltpu.VMEM((chunks, pols, ncyl, 2, feeds, LANES), bf16),
            pltpu.VMEM((ncyl, pols, 2, feeds), f32),
            pltpu.VMEM((ncyl * pols * 2, feeds, LANES), f32),
            pltpu.VMEM((ncyl, 2 * NS, 2 * feeds), bf16),
            pltpu.VMEM((2 * feeds, LANES), bf16),
            pltpu.VMEM((ncyl * pols, 2 * NS, LANES), bf16),
            pltpu.VMEM((2 + ncal, owners, 4 * NS // owners, LANES), f32),
            pltpu.VMEM((chunks, ncal, 8, LANES), f32),
            pltpu.VMEM((owners, 8, LANES), f32),
            pltpu.VMEM((owners, 8, LANES), f32),
            pltpu.VMEM((8, LANES), f32),
            pltpu.VMEM((nchan, 8, LANES), f32),
            dma((3, chunks, pols)),
            dma((chunks, pols, ncyl)),
            dma((3,)),
            dma((ncyl,)),
            dma((owners,)),
            dma((owners,)),
            dma((nchan,)),
            dma((nchan,)),
            pltpu.SemaphoreType.REGULAR((2,)),
        ],
        compiler_params=pltpu.CompilerParams(
            collective_id=0, has_side_effects=True, vmem_limit_bytes=60 * 1024 * 1024
        ),
    )(voltages, feed_gains, grid_slot, transit_start)
    span = NS // owners
    vmem = pl.BlockSpec(memory_space=pltpu.VMEM)
    return pl.pallas_call(
        place_outputs,
        out_shape=(
            jax.ShapeDtypeStruct((ch_dev, 4, span), f32),
            jax.ShapeDtypeStruct((ncal, 4, span), f32),
        ),
        in_specs=[vmem, vmem],
        out_specs=(vmem, vmem),
    )(beam_map, transit_snr)


def solution(mesh):
    in_specs = (
        P("chan", "cyl", None, None, None, "tm"),
        P("chan", "cyl", None, None, None),
        P(),
        P(),
    )
    out_specs = (P("chan", None, ("cyl", "tm")), P(None, None, ("cyl", "tm")))
    return jax.shard_map(
        per_device, mesh=mesh, in_specs=in_specs, out_specs=out_specs, check_vma=False
    )
```
